32 devices in a mesh: ga: 2 (over y), gx: 16 (over z, x, core).
Axes of the slice: x: 2, y: 2, z: 4, core: 2. Of those that a mesh axis runs over, the one named last changes fastest.
Arguments:
- fields: bfloat16 [2048, 512, 128], P('gx', 'ga'), parts along dimension 1, may hold values from -6 to 6
- cotangent: bfloat16 [2048, 512, 128], P('gx', 'ga'), parts along dimension 1, may hold values from -6 to 6
- point_weight: bfloat16 [128, 128], replicated, may hold values from -0.5 to 0.5
- mix_weight: bfloat16 [12, 128, 128], replicated, may hold values from -0.5 to 0.5
- bias_vec: bfloat16 [128], replicated, may hold values from -3 to 3
Outputs:
- grad_input: bfloat16 [2048, 512, 128], P('gx', 'ga'), parts along dimension 1
- grad_mix: bfloat16 [24, 128, 128], P('ga'), parts along dimension 0
- grad_point: bfloat16 [256, 128], P('ga'), parts along dimension 0
- grad_bias: bfloat16 [256], P('ga'), parts along dimension 0
The draws below stay inside these ranges and needn't reach their ends.
There are 2 independent parts, one for each index of `ga`. The reference program is written for one: setup_inputs(seed, part) draws one part's arguments, and reference() takes and returns one part's arrays. A program takes and returns all parts, laid end to end along the dimension named above; an argument that names none is the same for every part. Nothing has to cross between parts.
All inputs are finite; a program needn't handle non-finite values.
Results may differ from the reference program's by a relative error of at most 0.012.
Values sent between devices are 32-bit elements; how exact they have to be, the bound alone decides.
A program may use at most 128 MiB of HBM per device.

```python
import math
import jax
import jax.numpy as jnp
import numpy as np
from jax import lax

NX = 2048
C = 128
LEVELS = 11
NY = 256


def block_scale(key, extent, pieces, smallest, top_value):
    level, own = 1.0, jax.random.fold_in(key, 6)
    for position, shards_of in pieces:
        heights = jnp.exp(jax.random.uniform(jax.random.fold_in(own, position), (shards_of,), jnp.float32, smallest / len(pieces), top_value / len(pieces)))
        level = level * jnp.repeat(heights, extent[position] // shards_of).reshape([-1 if axis == position else 1 for axis in range(len(extent))])
    return level


def noise(key, shape, spread, most, split=(), held_as=jnp.bfloat16):
    values = jax.random.normal(key, shape, jnp.float32) * spread
    if len(split) > 0:
        values = block_scale(key, shape, split, -0.22, 0.18) * values
    return jnp.clip(values, min=-most, max=most).astype(held_as)


def setup_inputs(seed: int = 0, part: int = 0) -> dict:
    keys = jax.random.split(jax.random.key(seed), 6)
    part_keys = jax.random.split(jax.random.fold_in(keys[5], part), 6)
    fields = noise(part_keys[0], (NX, NY, C), 1.0, 6.0, ((0, 16),))
    cotangent = noise(part_keys[1], (NX, NY, C), 1.0, 6.0, ((0, 16),))
    point_weight = noise(keys[2], (C, C), C ** -0.5, 0.5)
    mix_weight = noise(keys[3], (LEVELS + 1, C, C), C ** -0.5, 0.5)
    bias_vec = noise(keys[4], (C,), 0.5, 3.0)
    return dict(fields=fields, cotangent=cotangent, point_weight=point_weight, mix_weight=mix_weight, bias_vec=bias_vec)


root_half = 0.7071067811865476

def haar_forward(signal, depth_count):
    for degree in range(depth_count):
        stride = 2 ** degree
        shaped = signal.reshape((signal.shape[0] // (2 * stride), 2, stride) + signal.shape[1:])
        even_rows = shaped[:, 0, 0]
        odd_rows = shaped[:, 1, 0]
        shaped = shaped.at[:, 0, 0].set((even_rows + odd_rows) * root_half)
        shaped = shaped.at[:, 1, 0].set((odd_rows - even_rows) * root_half)
        signal = shaped.reshape(signal.shape)
    return signal

def haar_inverse(signal, depth_count):
    for degree in reversed(range(depth_count)):
        stride = 2 ** degree
        shaped = signal.reshape((signal.shape[0] // (2 * stride), 2, stride) + signal.shape[1:])
        coarse_rows = shaped[:, 0, 0]
        detail_rows = shaped[:, 1, 0]
        shaped = shaped.at[:, 0, 0].set((coarse_rows - detail_rows) * root_half)
        shaped = shaped.at[:, 1, 0].set((coarse_rows + detail_rows) * root_half)
        signal = shaped.reshape(signal.shape)
    return signal

def mix_levels(coeffs_b, weights, depth_count, first_weight):
    output = jnp.zeros(coeffs_b.shape, jnp.float32)
    for degree in range(depth_count):
        stride = 2 ** degree
        picked = coeffs_b[stride::2 * stride]
        output = output.at[stride::2 * stride].set(jnp.dot(picked, weights[degree], preferred_element_type=jnp.float32))
    output = output.at[0].set(jnp.dot(coeffs_b[0], first_weight, preferred_element_type=jnp.float32))
    return output

def outer_sum(left, right):
    left_flat = left.reshape((-1, left.shape[-1]))
    right_flat = right.reshape((-1, right.shape[-1]))
    return lax.dot_general(left_flat, right_flat, (((0,), (0,)), ((), ())), preferred_element_type=jnp.float32)

def gelu_slope(pre_act, cotangent):
    unused_out, pullback = jax.vjp(jax.nn.gelu, pre_act)
    return pullback(cotangent.astype(pre_act.dtype))[0].astype(jnp.bfloat16)

def level_factors(columns):
    counts = [columns * NX / 2 ** (degree + 1) for degree in range(LEVELS)] + [columns]
    return np.array([1.0 / math.sqrt(value) for value in counts], np.float32)

def reference(fields, cotangent, point_weight, mix_weight, bias_vec):
    coeffs = haar_forward(fields.astype(jnp.float32), LEVELS)
    coeffs_b = coeffs.astype(jnp.bfloat16)
    mixed_rows = mix_levels(coeffs_b, mix_weight, LEVELS, mix_weight[LEVELS])
    spectral = haar_inverse(mixed_rows, LEVELS)
    pre_act = spectral + jnp.dot(fields, point_weight, preferred_element_type=jnp.float32) + bias_vec.astype(jnp.float32)
    slope_b = gelu_slope(pre_act, cotangent)
    back_coeffs = haar_forward(slope_b.astype(jnp.float32), LEVELS)
    back_b = back_coeffs.astype(jnp.bfloat16)
    grads_list = []
    for degree in range(LEVELS):
        stride = 2 ** degree
        grads_list.append(outer_sum(coeffs_b[stride::2 * stride], back_b[stride::2 * stride]))
    grads_list.append(outer_sum(coeffs_b[0:1], back_b[0:1]))
    factors = jnp.asarray(level_factors(fields.shape[1]))
    grad_mix = (jnp.stack(grads_list) * factors[:, None, None]).astype(jnp.bfloat16)
    scale_all = 1.0 / math.sqrt(NX * fields.shape[1])
    grad_point = (outer_sum(fields, slope_b) * scale_all).astype(jnp.bfloat16)
    grad_bias = (lax.optimization_barrier(jnp.sum(slope_b.astype(jnp.float32), axis=(0, 1))) * scale_all).astype(jnp.bfloat16)
    transposed = jnp.swapaxes(mix_weight, 1, 2)
    back_mixed = mix_levels(back_b, transposed, LEVELS, transposed[LEVELS])
    grad_input = (haar_inverse(back_mixed, LEVELS) + jnp.dot(slope_b, point_weight.T, preferred_element_type=jnp.float32)).astype(jnp.bfloat16)
    return (grad_input, grad_mix, grad_point, grad_bias)
```

```python
import functools
import math

import jax
import jax.numpy as jnp
import numpy as np
from jax import lax
from jax.experimental import pallas as pl
from jax.experimental.pallas import tpu as pltpu
from jax.sharding import PartitionSpec as P

F32 = jnp.float32
BF16 = jnp.bfloat16
LANES = 16
GELU_K = math.sqrt(2.0 / math.pi)
GELU_C = 0.044715


def offset(rows, level):
    return rows - (rows >> level)


def outer(left, right):
    return lax.dot_general(left, right, (((0,), (0,)), ((), ())), preferred_element_type=F32)


def slope_of(value, cot):
    square = value * value
    inner = value * (GELU_K + (GELU_K * GELU_C) * square)
    half = 0.5 + 0.5 * jnp.tanh(inner)
    ramp = value * (2.0 * GELU_K + (6.0 * GELU_K * GELU_C) * square)
    return cot * (half * (1.0 + (1.0 - half) * ramp))


def analyse_kernel(depth, fields_ref, coeff_ref, coarse_ref):
    rows = 1 << depth

    @pl.loop(0, fields_ref.shape[1] // LANES)
    def _(sub):
        cols = pl.ds(pl.multiple_of(sub * LANES, LANES), LANES)

        def tree(level, index):
            if level == 0:
                return fields_ref[index, cols, :].astype(F32)
            even = tree(level - 1, 2 * index)
            odd = tree(level - 1, 2 * index + 1)
            coeff_ref[0, offset(rows, level - 1) + index, cols, :] = (odd - even).astype(BF16)
            return even + odd

        coarse_ref[cols, :] = tree(depth, 0)


def mix_block(depth, coeff_ref, weight_ref, mixed_ref):
    rows = 1 << depth
    wide = coeff_ref.shape[2]
    for level in range(depth):
        first, count = offset(rows, level), rows >> (level + 1)
        flat = coeff_ref[0, first : first + count].reshape(count * wide, coeff_ref.shape[3])
        mixed_ref[first : first + count] = jnp.dot(
            flat, weight_ref[level], preferred_element_type=F32
        ).reshape(count, wide, weight_ref.shape[2])


def middle_kernel(
    depth, coeff_ref, cot_ref, coarse_ref, weight_ref, bias_ref, back_ref, sums_ref, grad_ref, mixed_ref
):
    rows = 1 << depth
    wide = coeff_ref.shape[2]
    mix_block(depth, coeff_ref, weight_ref, mixed_ref)

    @pl.loop(0, wide // LANES)
    def _(sub):
        cols = pl.ds(pl.multiple_of(sub * LANES, LANES), LANES)

        def tree(level, index, value):
            if level == 0:
                cot = cot_ref[index, cols, :].astype(F32)
                return slope_of(value, cot).astype(BF16).astype(F32)
            place = offset(rows, level - 1) + index
            detail = mixed_ref[place, cols, :]
            even = tree(level - 1, 2 * index, value - detail)
            odd = tree(level - 1, 2 * index + 1, value + detail)
            back_ref[0, place, cols, :] = (odd - even).astype(BF16)
            return even + odd

        sums_ref[cols, :] = tree(depth, 0, coarse_ref[cols, :] + bias_ref[0:1, :])

    @pl.when(pl.program_id(0) == 0)
    def _():
        grad_ref[...] = jnp.zeros_like(grad_ref)

    for level in range(depth):
        first, count = offset(rows, level), rows >> (level + 1)
        left = coeff_ref[0, first : first + count].reshape(count * wide, coeff_ref.shape[3])
        right = back_ref[0, first : first + count].reshape(count * wide, coeff_ref.shape[3])
        grad_ref[level] += outer(left, right)


def synth_kernel(depth, back_ref, coarse_ref, weight_ref, out_ref, mixed_ref):
    rows = 1 << depth
    mix_block(depth, back_ref, weight_ref, mixed_ref)

    @pl.loop(0, back_ref.shape[2] // LANES)
    def _(sub):
        cols = pl.ds(pl.multiple_of(sub * LANES, LANES), LANES)

        def tree(level, index, value):
            if level == 0:
                out_ref[index, cols, :] = value.astype(BF16)
                return
            detail = mixed_ref[offset(rows, level - 1) + index, cols, :]
            tree(level - 1, 2 * index, value - detail)
            tree(level - 1, 2 * index + 1, value + detail)

        tree(depth, 0, coarse_ref[cols, :])


def cross_kernel(
    count, with_grad, coarse_ref, weight_ref, other_ref, out_ref, coeff_ref, grad_ref,
    arrived, leaving, landed, send_a, recv_a, send_b, recv_b,
):
    me = lax.axis_index("gx")
    depth = count.bit_length() - 1
    cols, chans = coarse_ref.shape[1], coarse_ref.shape[2]
    barrier = pltpu.get_barrier_semaphore()

    def peer(step):
        return lax.rem(me + step, count)

    @pl.loop(1, count)
    def _(step):
        pl.semaphore_signal(
            barrier, inc=1, device_id={"gx": peer(step)}, device_id_type=pl.DeviceIdType.MESH
        )

    pl.semaphore_wait(barrier, count - 1)

    def swap(source, target, send, recv, step):
        return pltpu.make_async_remote_copy(
            src_ref=source.at[peer(step)],
            dst_ref=target.at[me],
            send_sem=send.at[step],
            recv_sem=recv.at[step],
            device_id={"gx": peer(step)},
            device_id_type=pl.DeviceIdType.MESH,
        )

    def exchange(source, target, send, recv):
        @pl.loop(1, count)
        def _(step):
            swap(source, target, send, recv, step).start()

        target[me] = source[me]

        @pl.loop(1, count)
        def _(step):
            swap(source, target, send, recv, step).wait()

    exchange(coarse_ref, arrived, send_a, recv_a)

    def down(level, index):
        if level == 0:
            return arrived[index]
        even = down(level - 1, 2 * index)
        odd = down(level - 1, 2 * index + 1)
        coeff_ref[offset(count, level - 1) + index] = (odd - even).astype(BF16)
        return even + odd

    coeff_ref[count - 1] = down(depth, 0).astype(BF16)
    mixed = []
    for level in range(depth + 1):
        first = offset(count, level)
        total = max(count >> (level + 1), 1)
        flat = coeff_ref[first : first + total].astype(F32).reshape(total * cols, chans).astype(BF16)
        mixed.append(
            jnp.dot(flat, weight_ref[level], preferred_element_type=F32).reshape(total, cols, chans)
        )
        if with_grad:
            prior = other_ref[first : first + total].astype(F32).reshape(total * cols, chans)
            grad_ref[level] = outer(prior.astype(BF16), flat)

    def up(level, index, value):
        if level == 0:
            leaving[index] = value
            return
        detail = mixed[level - 1][index]
        up(level - 1, 2 * index, value - detail)
        up(level - 1, 2 * index + 1, value + detail)

    up(depth, 0, mixed[depth][0])
    exchange(leaving, landed, send_b, recv_b)
    out_ref[...] = landed[...]


def cross(coarse, weights, other, with_grad, identity):
    count, cols, chans = coarse.shape
    levels = weights.shape[0]
    grad_shape = (levels if with_grad else 1, 8 if not with_grad else chans, chans)
    whole = pl.BlockSpec(memory_space=pltpu.VMEM)
    return pl.pallas_call(
        functools.partial(cross_kernel, count, with_grad),
        out_shape=(
            jax.ShapeDtypeStruct(coarse.shape, F32),
            jax.ShapeDtypeStruct(coarse.shape, BF16),
            jax.ShapeDtypeStruct(grad_shape, F32),
        ),
        in_specs=[whole] * 3,
        out_specs=(whole,) * 3,
        scratch_shapes=[pltpu.VMEM(coarse.shape, F32)] * 3 + [pltpu.SemaphoreType.DMA((count,))] * 4,
        compiler_params=pltpu.CompilerParams(
            collective_id=identity, has_side_effects=True, vmem_limit_bytes=32 << 20
        ),
    )(coarse, weights, other)


def shards(fields, cotangent, point_weight, mix_weight, bias_vec):
    rows, width, chans = fields.shape
    depth = rows.bit_length() - 1
    count = lax.axis_size("gx")
    levels = mix_weight.shape[0]
    step = 32
    blocks = width // step
    scales = [2.0 ** -(level + 1) for level in range(levels - 1)] + [2.0 ** -(levels - 1)]
    scales = np.array(scales, np.float32)
    joined = mix_weight.astype(F32) + point_weight.astype(F32)[None]
    weights = (joined * scales[:, None, None]).astype(BF16)
    turned = jnp.swapaxes(weights, 1, 2)
    bias = jnp.broadcast_to(bias_vec.astype(F32)[None], (8, chans))

    field_spec = pl.BlockSpec((rows, step, chans), lambda i: (0, i, 0))
    coeff_spec = pl.BlockSpec((1, rows, step, chans), lambda i: (i, 0, 0, 0))
    row_spec = pl.BlockSpec((step, chans), lambda i: (i, 0))
    weight_spec = pl.BlockSpec((depth, chans, chans), lambda i: (0, 0, 0))
    params = pltpu.CompilerParams(
        dimension_semantics=("arbitrary",), vmem_limit_bytes=48 << 20
    )
    coeff_type = jax.ShapeDtypeStruct((blocks, rows, step, chans), BF16)
    row_type = jax.ShapeDtypeStruct((width, chans), F32)
    mixed_type = pltpu.VMEM((rows, step, chans), F32)

    coeffs, coarse = pl.pallas_call(
        functools.partial(analyse_kernel, depth),
        grid=(blocks,),
        in_specs=[field_spec],
        out_specs=(coeff_spec, row_spec),
        out_shape=(coeff_type, row_type),
        compiler_params=params,
    )(fields)

    far_shape = (count, width // count, chans)
    local_w, far_w = weights[:depth], weights[depth:]
    local_t, far_t = turned[:depth], turned[depth:]
    spectral, far_coeffs, _ = cross(
        coarse.reshape(far_shape), far_w, jnp.zeros((1, 16, chans), BF16), False, 0
    )

    backs, sums, grad_local = pl.pallas_call(
        functools.partial(middle_kernel, depth),
        grid=(blocks,),
        in_specs=[
            coeff_spec, field_spec, row_spec, weight_spec,
            pl.BlockSpec((8, chans), lambda i: (0, 0)),
        ],
        out_specs=(coeff_spec, row_spec, weight_spec),
        out_shape=(coeff_type, row_type, jax.ShapeDtypeStruct((depth, chans, chans), F32)),
        scratch_shapes=[mixed_type],
        compiler_params=params,
    )(coeffs, cotangent, spectral.reshape(width, chans), local_w, bias)

    spectral_back, _, grad_far = cross(sums.reshape(far_shape), far_t, far_coeffs, True, 1)

    bias_local = jnp.sum(sums.reshape(width // 8, 8, chans), axis=0)
    grads = jnp.concatenate([grad_local, grad_far], axis=0).reshape(levels * chans, chans)
    totals = lax.psum(jnp.concatenate([grads, bias_local], axis=0), "gx")

    (grad_input,) = pl.pallas_call(
        functools.partial(synth_kernel, depth),
        grid=(blocks,),
        in_specs=[coeff_spec, row_spec, weight_spec],
        out_specs=(field_spec,),
        out_shape=(jax.ShapeDtypeStruct(fields.shape, BF16),),
        scratch_shapes=[mixed_type],
        compiler_params=params,
        cost_estimate=pl.CostEstimate(
            flops=2 * rows * width * chans * chans, bytes_accessed=4 * rows * width * chans,
            transcendentals=0,
        ),
    )(backs, spectral_back.reshape(width, chans), local_t)

    total_rows = rows * count
    raw = totals[: levels * chans].reshape(levels, chans, chans) * scales[:, None, None]
    members = [width * total_rows / 2 ** (level + 1) for level in range(levels - 1)] + [width]
    factors = np.array([1.0 / math.sqrt(value) for value in members], np.float32)
    scale_all = 1.0 / math.sqrt(total_rows * width)
    grad_mix = (raw * factors[:, None, None]).astype(BF16)
    grad_point = (jnp.sum(raw, axis=0) * scale_all).astype(BF16)
    grad_bias = (jnp.sum(totals[levels * chans :], axis=0) * scale_all).astype(BF16)
    return (grad_input, grad_mix, grad_point, grad_bias)


def solution(mesh):
    in_specs = (P("gx", "ga", None), P("gx", "ga", None), P(), P(), P())
    out_specs = (P("gx", "ga", None), P("ga", None, None), P("ga", None), P("ga"))
    return jax.shard_map(shards, mesh=mesh, in_specs=in_specs, out_specs=out_specs, check_vma=False)
```

```python
import functools
import math

import jax
import jax.numpy as jnp
import numpy as np
from jax import lax
from jax.experimental import pallas as pl
from jax.experimental.pallas import tpu as pltpu
from jax.sharding import PartitionSpec as P

F32 = jnp.float32
BF16 = jnp.bfloat16
LANES = 16
GELU_K = math.sqrt(2.0 / math.pi)
GELU_C = 0.044715


def offset(rows, level):
    return rows - (rows >> level)


def outer(left, right):
    return lax.dot_general(left, right, (((0,), (0,)), ((), ())), preferred_element_type=F32)


def apply_weight(rows, weight, turned):
    sides = (((1,), (1 if turned else 0,)), ((), ()))
    return lax.dot_general(rows, weight, sides, preferred_element_type=F32)


def slope_of(value, cot):
    square = value * value
    inner = value * (GELU_K + (GELU_K * GELU_C) * square)
    half = 0.5 + 0.5 * jnp.tanh(inner)
    ramp = value * (2.0 * GELU_K + (6.0 * GELU_K * GELU_C) * square)
    return cot * (half * (1.0 + (1.0 - half) * ramp))


def analyse_kernel(depth, fields_ref, coeff_ref, coarse_ref):
    rows = 1 << depth

    @pl.loop(0, fields_ref.shape[1] // LANES)
    def _(sub):
        cols = pl.ds(pl.multiple_of(sub * LANES, LANES), LANES)

        def tree(level, index):
            if level == 0:
                return fields_ref[index, cols, :].astype(F32)
            even = tree(level - 1, 2 * index)
            odd = tree(level - 1, 2 * index + 1)
            coeff_ref[0, offset(rows, level - 1) + index, cols, :] = (odd - even).astype(BF16)
            return even + odd

        coarse_ref[cols, :] = tree(depth, 0)


def mix_block(depth, coeff_ref, weight_ref, mixed_ref, turned):
    rows = 1 << depth
    wide = coeff_ref.shape[2]
    for level in range(depth):
        first, count = offset(rows, level), rows >> (level + 1)
        flat = coeff_ref[0, first : first + count].reshape(count * wide, coeff_ref.shape[3])
        mixed_ref[first : first + count] = apply_weight(flat, weight_ref[level], turned).reshape(
            count, wide, weight_ref.shape[2]
        )


def middle_kernel(
    depth, coeff_ref, cot_ref, coarse_ref, weight_ref, bias_ref, back_ref, sums_ref, grad_ref, mixed_ref
):
    rows = 1 << depth
    wide = coeff_ref.shape[2]
    mix_block(depth, coeff_ref, weight_ref, mixed_ref, False)

    @pl.loop(0, wide // LANES)
    def _(sub):
        cols = pl.ds(pl.multiple_of(sub * LANES, LANES), LANES)

        def tree(level, index, value):
            if level == 0:
                cot = cot_ref[index, cols, :].astype(F32)
                return slope_of(value, cot).astype(BF16).astype(F32)
            place = offset(rows, level - 1) + index
            detail = mixed_ref[place, cols, :]
            even = tree(level - 1, 2 * index, value - detail)
            odd = tree(level - 1, 2 * index + 1, value + detail)
            back_ref[0, place, cols, :] = (odd - even).astype(BF16)
            return even + odd

        sums_ref[cols, :] = tree(depth, 0, coarse_ref[cols, :] + bias_ref[0:1, :])

    @pl.when(pl.program_id(0) == 0)
    def _():
        grad_ref[...] = jnp.zeros_like(grad_ref)

    for level in range(depth):
        first, count = offset(rows, level), rows >> (level + 1)
        left = coeff_ref[0, first : first + count].reshape(count * wide, coeff_ref.shape[3])
        right = back_ref[0, first : first + count].reshape(count * wide, coeff_ref.shape[3])
        grad_ref[level] += outer(left, right)


def synth_kernel(depth, back_ref, coarse_ref, weight_ref, out_ref, mixed_ref):
    rows = 1 << depth
    mix_block(depth, back_ref, weight_ref, mixed_ref, True)

    @pl.loop(0, back_ref.shape[2] // LANES)
    def _(sub):
        cols = pl.ds(pl.multiple_of(sub * LANES, LANES), LANES)

        def tree(level, index, value):
            if level == 0:
                out_ref[index, cols, :] = value.astype(BF16)
                return
            detail = mixed_ref[offset(rows, level - 1) + index, cols, :]
            tree(level - 1, 2 * index, value - detail)
            tree(level - 1, 2 * index + 1, value + detail)

        tree(depth, 0, coarse_ref[cols, :])


class Stream:
    def __init__(self, total, slots, result, send, recv, bits, me):
        self.total, self.slots, self.result = total, slots, result
        self.send, self.recv = send, recv
        start, length, place = 0, total.shape[0], 0
        self.plan = []
        for turn, bit in enumerate(bits):
            upper = lax.rem(me // (1 << bit), 2)
            partner = me + (1 - 2 * upper) * (1 << bit)
            halved = length % 2 == 0
            size = length // 2 if halved else length
            keep = start + upper * size if halved else start
            give = start + (1 - upper) * size if halved else start
            self.plan.append((turn, partner, halved, size, keep, give, place))
            start, length, place = keep, size, place + size
        self.stages = [("sum",) + item for item in self.plan]
        self.stages += [("spread",) + item for item in self.plan[::-1] if item[2]]

    def copy(self, index):
        kind, turn, partner, halved, size, keep, give, place = self.stages[index]
        if kind == "sum":
            source = self.total.at[pl.ds(give, size)]
            target = self.slots.at[pl.ds(place, size)]
        else:
            source = self.result.at[pl.ds(keep, size)]
            target = self.result.at[pl.ds(keep, size)]
        return pltpu.make_async_remote_copy(
            src_ref=source,
            dst_ref=target,
            send_sem=self.send.at[index],
            recv_sem=self.recv.at[index],
            device_id={"gx": partner},
            device_id_type=pl.DeviceIdType.MESH,
        )

    def start(self, index):
        if index < len(self.stages):
            self.copy(index).start()

    def finish(self, index):
        self.copy(index).wait()
        kind, turn, partner, halved, size, keep, give, place = self.stages[index]
        if kind == "sum":
            here = pl.ds(keep, size)
            into = self.result if turn == len(self.plan) - 1 else self.total
            into[here] = self.total[here] + self.slots[pl.ds(place, size)]


def slot_tiles(tiles, count):
    used = 0
    for _ in range(count.bit_length() - 1):
        tiles = tiles // 2 if tiles % 2 == 0 else tiles
        used += tiles
    return used


def far_levels(count, first_level, arrived, coeff_ref, weight_ref, turned):
    depth = count.bit_length() - 1
    cols, chans = arrived.shape[1], arrived.shape[2]

    def down(level, index):
        if level == 0:
            return arrived[index]
        even = down(level - 1, 2 * index)
        odd = down(level - 1, 2 * index + 1)
        coeff_ref[offset(count, level - 1) + index] = (odd - even).astype(BF16)
        return even + odd

    coeff_ref[count - 1] = down(depth, 0).astype(BF16)
    mixed, flats = [], []
    for level in range(depth + 1):
        first = offset(count, level)
        total = max(count >> (level + 1), 1)
        flat = coeff_ref[first : first + total].astype(F32).reshape(total * cols, chans).astype(BF16)
        flats.append(flat)
        mixed.append(
            apply_weight(flat, weight_ref[first_level + level], turned).reshape(total, cols, chans)
        )
    return mixed, flats


def far_back(count, mixed, leaving, cols):
    depth = count.bit_length() - 1

    def up(level, index, value):
        if level == 0:
            leaving[index, 0:cols] = value
            return
        detail = mixed[level - 1][index]
        up(level - 1, 2 * index, value - detail)
        up(level - 1, 2 * index + 1, value + detail)

    up(depth, 0, mixed[depth][0])


def greet(count, me):
    barrier = pltpu.get_barrier_semaphore()

    @pl.loop(1, count)
    def _(step):
        pl.semaphore_signal(
            barrier,
            inc=1,
            device_id={"gx": lax.rem(me + step, count)},
            device_id_type=pl.DeviceIdType.MESH,
        )

    pl.semaphore_wait(barrier, count - 1)


def swap(count, me, source, target, send, recv, step):
    peer = lax.rem(me + step, count)
    return pltpu.make_async_remote_copy(
        src_ref=source.at[peer],
        dst_ref=target.at[me],
        send_sem=send.at[step],
        recv_sem=recv.at[step],
        device_id={"gx": peer},
        device_id_type=pl.DeviceIdType.MESH,
    )


def exchange_start(count, me, source, target, send, recv):
    @pl.loop(1, count)
    def _(step):
        swap(count, me, source, target, send, recv, step).start()

    target[me] = source[me]


def exchange_wait(count, me, source, target, send, recv):
    @pl.loop(1, count)
    def _(step):
        swap(count, me, source, target, send, recv, step).wait()


def cross_kernel(
    count, first_level, coarse_ref, weight_ref, out_ref, coeff_ref,
    arrived, leaving, landed, send_a, recv_a, send_b, recv_b,
):
    me = lax.axis_index("gx")
    greet(count, me)
    exchange_start(count, me, coarse_ref, arrived, send_a, recv_a)
    exchange_wait(count, me, coarse_ref, arrived, send_a, recv_a)
    mixed, _ = far_levels(count, first_level, arrived, coeff_ref, weight_ref, False)
    far_back(count, mixed, leaving, coarse_ref.shape[1])
    exchange_start(count, me, leaving, landed, send_b, recv_b)
    exchange_wait(count, me, leaving, landed, send_b, recv_b)
    out_ref[...] = landed[...]


def cross_back_kernel(
    count, first_level, factors, scales, scale_all, coarse_ref, weight_ref, other_ref, local_ref,
    out_ref, mix_ref, point_ref, bias_ref,
    coeff_ref, arrived, leaving, landed, near, near_slots, near_sum, far, far_slots, far_sum,
    send_a, recv_a, send_b, recv_b, send_n, recv_n, send_f, recv_f,
):
    me = lax.axis_index("gx")
    cols, chans = coarse_ref.shape[1], coarse_ref.shape[2]
    tiles = chans // 8
    bits = list(range(count.bit_length() - 1))
    greet(count, me)
    exchange_start(count, me, coarse_ref, arrived, send_a, recv_a)
    near[...] = local_ref[...]
    streams = [Stream(near, near_slots, near_sum, send_n, recv_n, bits, me)]
    streams.append(Stream(far, far_slots, far_sum, send_f, recv_f, bits[:1] + bits[2:] + bits[1:2], me))
    streams[0].start(0)
    exchange_wait(count, me, coarse_ref, arrived, send_a, recv_a)
    mixed, flats = far_levels(count, first_level, arrived, coeff_ref, weight_ref, True)
    far_back(count, mixed, leaving, cols)
    part = jnp.sum(jnp.sum(arrived[...], axis=0), axis=0, keepdims=True)
    leaving[:, cols:] = jnp.broadcast_to(part[None], (count, leaving.shape[1] - cols, chans))
    exchange_start(count, me, leaving, landed, send_b, recv_b)
    for level, flat in enumerate(flats):
        first = offset(count, level)
        total = max(count >> (level + 1), 1)
        prior = other_ref[first : first + total].astype(F32).reshape(total * cols, chans)
        far[level * tiles : (level + 1) * tiles] = outer(prior.astype(BF16), flat).reshape(
            tiles, 8, chans
        )
    streams[1].start(0)
    for index in range(max(len(stream.stages) for stream in streams)):
        for stream in streams:
            if index < len(stream.stages):
                stream.finish(index)
                stream.start(index + 1)
    exchange_wait(count, me, leaving, landed, send_b, recv_b)
    out_ref[...] = landed[:, 0:cols]
    bias_ref[...] = jnp.sum(landed[:, cols : cols + 8], axis=0) * scale_all
    point = jnp.zeros((chans, chans), F32)
    for level in range(len(scales)):
        source, base = (near_sum, level)
        if level >= first_level:
            source, base = (far_sum, level - first_level)
        raw = source[base * tiles : (base + 1) * tiles].reshape(chans, chans) * scales[level]
        mix_ref[level] = (raw * factors[level]).astype(BF16)
        point = point + raw
    point_ref[...] = (point * scale_all).astype(BF16)


def cross(coarse, weights, first_level):
    count, cols, chans = coarse.shape
    whole = pl.BlockSpec(memory_space=pltpu.VMEM)
    return pl.pallas_call(
        functools.partial(cross_kernel, count, first_level),
        out_shape=(
            jax.ShapeDtypeStruct(coarse.shape, F32),
            jax.ShapeDtypeStruct(coarse.shape, BF16),
        ),
        in_specs=[whole] * 2,
        out_specs=(whole,) * 2,
        scratch_shapes=[pltpu.VMEM(coarse.shape, F32)] * 3 + [pltpu.SemaphoreType.DMA((count,))] * 4,
        compiler_params=pltpu.CompilerParams(
            collective_id=0, has_side_effects=True, vmem_limit_bytes=32 << 20
        ),
    )(coarse, weights)


def cross_back(coarse, weights, other, local, first_level, factors, scales, scale_all):
    count, cols, chans = coarse.shape
    levels = weights.shape[0]
    whole = pl.BlockSpec(memory_space=pltpu.VMEM)
    tiles = chans // 8
    near, far = first_level * tiles, (levels - first_level) * tiles
    depth = count.bit_length() - 1
    padded = (count, cols + 8, chans)
    return pl.pallas_call(
        functools.partial(cross_back_kernel, count, first_level, factors, scales, scale_all),
        out_shape=(
            jax.ShapeDtypeStruct(coarse.shape, F32),
            jax.ShapeDtypeStruct(weights.shape, BF16),
            jax.ShapeDtypeStruct((chans, chans), BF16),
            jax.ShapeDtypeStruct((8, chans), F32),
        ),
        in_specs=[whole] * 4,
        out_specs=(whole,) * 4,
        scratch_shapes=[
            pltpu.VMEM(coarse.shape, BF16),
            pltpu.VMEM(coarse.shape, F32),
            pltpu.VMEM(padded, F32),
            pltpu.VMEM(padded, F32),
            pltpu.VMEM((near, 8, chans), F32),
            pltpu.VMEM((slot_tiles(near, count), 8, chans), F32),
            pltpu.VMEM((near, 8, chans), F32),
            pltpu.VMEM((far, 8, chans), F32),
            pltpu.VMEM((slot_tiles(far, count), 8, chans), F32),
            pltpu.VMEM((far, 8, chans), F32),
        ]
        + [pltpu.SemaphoreType.DMA((count,))] * 4
        + [pltpu.SemaphoreType.DMA((2 * depth,))] * 4,
        compiler_params=pltpu.CompilerParams(
            collective_id=1, has_side_effects=True, vmem_limit_bytes=32 << 20
        ),
    )(coarse, weights, other, local.reshape(near, 8, chans))


def shards(fields, cotangent, point_weight, mix_weight, bias_vec):
    rows, width, chans = fields.shape
    depth = rows.bit_length() - 1
    count = lax.axis_size("gx")
    levels = mix_weight.shape[0]
    step = 32
    blocks = width // step
    scales = [2.0 ** -(level + 1) for level in range(levels - 1)] + [2.0 ** -(levels - 1)]
    scales = np.array(scales, np.float32)
    joined = mix_weight.astype(F32) + point_weight.astype(F32)[None]
    weights = (joined * scales[:, None, None]).astype(BF16)
    bias = jnp.broadcast_to(bias_vec.astype(F32)[None], (8, chans))

    field_spec = pl.BlockSpec((rows, step, chans), lambda i: (0, i, 0))
    coeff_spec = pl.BlockSpec((1, rows, step, chans), lambda i: (i, 0, 0, 0))
    row_spec = pl.BlockSpec((step, chans), lambda i: (i, 0))
    weight_spec = pl.BlockSpec((levels, chans, chans), lambda i: (0, 0, 0))
    grad_spec = pl.BlockSpec((depth, chans, chans), lambda i: (0, 0, 0))
    params = pltpu.CompilerParams(
        dimension_semantics=("arbitrary",), vmem_limit_bytes=48 << 20
    )
    coeff_type = jax.ShapeDtypeStruct((blocks, rows, step, chans), BF16)
    row_type = jax.ShapeDtypeStruct((width, chans), F32)
    mixed_type = pltpu.VMEM((rows, step, chans), F32)

    coeffs, coarse = pl.pallas_call(
        functools.partial(analyse_kernel, depth),
        grid=(blocks,),
        in_specs=[field_spec],
        out_specs=(coeff_spec, row_spec),
        out_shape=(coeff_type, row_type),
        compiler_params=params,
    )(fields)

    far_shape = (count, width // count, chans)
    spectral, far_coeffs = cross(coarse.reshape(far_shape), weights, depth)

    backs, sums, grad_local = pl.pallas_call(
        functools.partial(middle_kernel, depth),
        grid=(blocks,),
        in_specs=[
            coeff_spec, field_spec, row_spec, weight_spec,
            pl.BlockSpec((8, chans), lambda i: (0, 0)),
        ],
        out_specs=(coeff_spec, row_spec, grad_spec),
        out_shape=(coeff_type, row_type, jax.ShapeDtypeStruct((depth, chans, chans), F32)),
        scratch_shapes=[mixed_type],
        compiler_params=params,
    )(coeffs, cotangent, spectral.reshape(width, chans), weights, bias)

    total_rows = rows * count
    members = [width * total_rows / 2 ** (level + 1) for level in range(levels - 1)] + [width]
    factors = [1.0 / math.sqrt(value) for value in members]
    scale_all = 1.0 / math.sqrt(total_rows * width)
    spectral_back, grad_mix, grad_point, grad_bias = cross_back(
        sums.reshape(far_shape), weights, far_coeffs, grad_local, depth,
        factors, [float(value) for value in scales], scale_all,
    )

    (grad_input,) = pl.pallas_call(
        functools.partial(synth_kernel, depth),
        grid=(blocks,),
        in_specs=[coeff_spec, row_spec, weight_spec],
        out_specs=(field_spec,),
        out_shape=(jax.ShapeDtypeStruct(fields.shape, BF16),),
        scratch_shapes=[mixed_type],
        compiler_params=params,
        cost_estimate=pl.CostEstimate(
            flops=2 * rows * width * chans * chans, bytes_accessed=4 * rows * width * chans,
            transcendentals=0,
        ),
    )(backs, spectral_back.reshape(width, chans), weights)

    grad_bias = grad_bias[0].astype(BF16)
    return (grad_input, grad_mix, grad_point, grad_bias)


def solution(mesh):
    in_specs = (P("gx", "ga", None), P("gx", "ga", None), P(), P(), P())
    out_specs = (P("gx", "ga", None), P("ga", None, None), P("ga", None), P("ga"))
    return jax.shard_map(shards, mesh=mesh, in_specs=in_specs, out_specs=out_specs, check_vma=False)
```

```python
import functools
import math

import jax
import jax.numpy as jnp
import numpy as np
from jax import lax
from jax.experimental import pallas as pl
from jax.experimental.pallas import tpu as pltpu
from jax.sharding import PartitionSpec as P

F32 = jnp.float32
BF16 = jnp.bfloat16
LANES = 16
GELU_K = math.sqrt(2.0 / math.pi)
GELU_C = 0.044715


def offset(rows, level):
    return rows - (rows >> level)


def outer(left, right):
    return lax.dot_general(left, right, (((0,), (0,)), ((), ())), preferred_element_type=F32)


def apply_weight(rows, weight, turned):
    sides = (((1,), (1 if turned else 0,)), ((), ()))
    return lax.dot_general(rows, weight, sides, preferred_element_type=F32)


def slope_of(value, cot):
    square = value * value
    inner = value * (GELU_K + (GELU_K * GELU_C) * square)
    half = 0.5 + 0.5 * jnp.tanh(inner)
    ramp = value * (2.0 * GELU_K + (6.0 * GELU_K * GELU_C) * square)
    return cot * (half * (1.0 + (1.0 - half) * ramp))


def mix_block(depth, coeff_ref, weight_ref, mixed_ref, turned):
    rows = 1 << depth
    wide = coeff_ref.shape[1]
    for level in range(depth):
        first, count = offset(rows, level), rows >> (level + 1)
        flat = coeff_ref[first : first + count].reshape(count * wide, coeff_ref.shape[2])
        mixed_ref[first : first + count] = apply_weight(flat, weight_ref[level], turned).reshape(
            count, wide, weight_ref.shape[2]
        )


def synth_kernel(depth, back_ref, coarse_ref, weight_ref, out_ref, mixed_ref):
    rows = 1 << depth
    mix_block(depth, back_ref.at[0], weight_ref, mixed_ref, True)

    @pl.loop(0, back_ref.shape[2] // LANES)
    def _(sub):
        cols = pl.ds(pl.multiple_of(sub * LANES, LANES), LANES)

        def tree(level, index, value):
            if level == 0:
                out_ref[index, cols, :] = value.astype(BF16)
                return
            detail = mixed_ref[offset(rows, level - 1) + index, cols, :]
            tree(level - 1, 2 * index, value - detail)
            tree(level - 1, 2 * index + 1, value + detail)

        tree(depth, 0, coarse_ref[cols, :])


class Stream:
    def __init__(self, total, slots, result, send, recv, bits, me):
        self.total, self.slots, self.result = total, slots, result
        self.send, self.recv = send, recv
        start, length, place = 0, total.shape[0], 0
        self.plan = []
        for turn, bit in enumerate(bits):
            upper = lax.rem(me // (1 << bit), 2)
            partner = me + (1 - 2 * upper) * (1 << bit)
            halved = length % 2 == 0
            size = length // 2 if halved else length
            keep = start + upper * size if halved else start
            give = start + (1 - upper) * size if halved else start
            self.plan.append((turn, partner, halved, size, keep, give, place))
            start, length, place = keep, size, place + size
        self.stages = [("sum",) + item for item in self.plan]
        self.stages += [("spread",) + item for item in self.plan[::-1] if item[2]]

    def copy(self, index):
        kind, turn, partner, halved, size, keep, give, place = self.stages[index]
        if kind == "sum":
            source = self.total.at[pl.ds(give, size)]
            target = self.slots.at[pl.ds(place, size)]
        else:
            source = self.result.at[pl.ds(keep, size)]
            target = self.result.at[pl.ds(keep, size)]
        return pltpu.make_async_remote_copy(
            src_ref=source,
            dst_ref=target,
            send_sem=self.send.at[index],
            recv_sem=self.recv.at[index],
            device_id={"gx": partner},
            device_id_type=pl.DeviceIdType.MESH,
        )

    def start(self, index):
        if index < len(self.stages):
            self.copy(index).start()

    def finish(self, index):
        self.copy(index).wait()
        kind, turn, partner, halved, size, keep, give, place = self.stages[index]
        if kind == "sum":
            here = pl.ds(keep, size)
            into = self.result if turn == len(self.plan) - 1 else self.total
            into[here] = self.total[here] + self.slots[pl.ds(place, size)]


def slot_tiles(tiles, count):
    used = 0
    for _ in range(count.bit_length() - 1):
        tiles = tiles // 2 if tiles % 2 == 0 else tiles
        used += tiles
    return used


def far_levels(count, first_level, arrived, coeff_ref, weight_ref, turned):
    depth = count.bit_length() - 1
    cols, chans = arrived.shape[1], arrived.shape[2]

    def down(level, index):
        if level == 0:
            return arrived[index]
        even = down(level - 1, 2 * index)
        odd = down(level - 1, 2 * index + 1)
        coeff_ref[offset(count, level - 1) + index] = (odd - even).astype(BF16)
        return even + odd

    coeff_ref[count - 1] = down(depth, 0).astype(BF16)
    mixed, flats = [], []
    for level in range(depth + 1):
        first = offset(count, level)
        total = max(count >> (level + 1), 1)
        flat = coeff_ref[first : first + total].astype(F32).reshape(total * cols, chans).astype(BF16)
        flats.append(flat)
        mixed.append(
            apply_weight(flat, weight_ref[first_level + level], turned).reshape(total, cols, chans)
        )
    return mixed, flats


def far_back(count, mixed, leaving, cols):
    depth = count.bit_length() - 1

    def up(level, index, value):
        if level == 0:
            leaving[index, 0:cols] = value
            return
        detail = mixed[level - 1][index]
        up(level - 1, 2 * index, value - detail)
        up(level - 1, 2 * index + 1, value + detail)

    up(depth, 0, mixed[depth][0])


def swap(count, me, source, target, send, recv, step):
    peer = lax.rem(me + step, count)
    return pltpu.make_async_remote_copy(
        src_ref=source.at[peer],
        dst_ref=target.at[me],
        send_sem=send.at[step],
        recv_sem=recv.at[step],
        device_id={"gx": peer},
        device_id_type=pl.DeviceIdType.MESH,
    )


def exchange_start(count, me, source, target, send, recv):
    @pl.loop(1, count)
    def _(step):
        swap(count, me, source, target, send, recv, step).start()

    target[me] = source[me]


def exchange_wait(count, me, source, target, send, recv):
    @pl.loop(1, count)
    def _(step):
        swap(count, me, source, target, send, recv, step).wait()


def send_block(count, me, block, share, source, target, send, recv):
    @pl.loop(0, share)
    def _(turn):
        step = lax.rem(block * share + turn - me + count, count)

        @pl.when(step > 0)
        def _():
            swap(count, me, source, target, send, recv, step).start()


def main_kernel(
    count, depth, factors, scales, scale_all,
    fields_ref, cot_ref, weight_ref, bias_ref,
    back_ref, out_ref, mix_ref, point_ref, gbias_ref,
    coeff, mixed_all, far_coeff, far_scratch,
    source_a, arrived_a, leaving_a, landed_a,
    source_b, arrived_b, leaving_b, landed_b,
    near, near_slots, near_sum, far, far_slots, far_sum,
    send_a, recv_a, send_b, recv_b, send_c, recv_c, send_d, recv_d,
    send_n, recv_n, send_f, recv_f,
):
    me = lax.axis_index("gx")
    turn = pl.program_id(0)
    blocks, rows, wide, chans = coeff.shape
    cols = source_a.shape[1]
    tiles = chans // 8
    share, piece = wide // cols, LANES // cols
    bits = list(range(count.bit_length() - 1))
    barrier = pltpu.get_barrier_semaphore()

    @pl.when(turn == 0)
    def _():
        @pl.loop(1, count)
        def _(step):
            pl.semaphore_signal(
                barrier,
                inc=1,
                device_id={"gx": lax.rem(me + step, count)},
                device_id_type=pl.DeviceIdType.MESH,
            )

        near[...] = jnp.zeros_like(near)

    @pl.when(turn < blocks)
    def _():
        @pl.loop(0, wide // LANES)
        def _(sub):
            here = pl.ds(pl.multiple_of(sub * LANES, LANES), LANES)

            def tree(level, index):
                if level == 0:
                    return fields_ref[index, here, :].astype(F32)
                even = tree(level - 1, 2 * index)
                odd = tree(level - 1, 2 * index + 1)
                coeff[turn, offset(rows, level - 1) + index, here, :] = (odd - even).astype(BF16)
                return even + odd

            source_a[pl.ds(turn * share + sub * piece, piece)] = tree(depth, 0).reshape(
                piece, cols, chans
            )

        @pl.when(turn == 0)
        def _():
            pl.semaphore_wait(barrier, count - 1)

        send_block(count, me, turn, share, source_a, arrived_a, send_a, recv_a)

    @pl.when(turn == blocks)
    def _():
        @pl.loop(0, blocks // 2)
        def _(block):
            mix_block(depth, coeff.at[block], weight_ref, mixed_all.at[block], False)

        arrived_a[me] = source_a[me]
        exchange_wait(count, me, source_a, arrived_a, send_a, recv_a)
        mixed, _ = far_levels(count, depth, arrived_a, far_coeff, weight_ref, False)
        far_back(count, mixed, leaving_a, cols)
        exchange_start(count, me, leaving_a, landed_a, send_b, recv_b)

        @pl.loop(blocks // 2, blocks)
        def _(block):
            mix_block(depth, coeff.at[block], weight_ref, mixed_all.at[block], False)

        exchange_wait(count, me, leaving_a, landed_a, send_b, recv_b)

    @pl.when(turn >= blocks)
    def _():
        block = turn - blocks

        @pl.loop(0, wide // LANES)
        def _(sub):
            here = pl.ds(pl.multiple_of(sub * LANES, LANES), LANES)

            def tree(level, index, value):
                if level == 0:
                    cot = cot_ref[index, here, :].astype(F32)
                    return slope_of(value, cot).astype(BF16).astype(F32)
                place = offset(rows, level - 1) + index
                detail = mixed_all[block, place, here, :]
                even = tree(level - 1, 2 * index, value - detail)
                odd = tree(level - 1, 2 * index + 1, value + detail)
                back_ref[0, place, here, :] = (odd - even).astype(BF16)
                return even + odd

            pieces = pl.ds(block * share + sub * piece, piece)
            start = landed_a[pieces].reshape(LANES, chans) + bias_ref[0:1, :]
            source_b[pieces] = tree(depth, 0, start).reshape(piece, cols, chans)

        send_block(count, me, block, share, source_b, arrived_b, send_c, recv_c)
        for level in range(depth):
            first, number = offset(rows, level), rows >> (level + 1)
            left = coeff[block, first : first + number].reshape(number * wide, chans)
            right = back_ref[0, first : first + number].reshape(number * wide, chans)
            near[level * tiles : (level + 1) * tiles] += outer(left, right).reshape(tiles, 8, chans)

    @pl.when(turn == 2 * blocks - 1)
    def _():
        streams = [Stream(near, near_slots, near_sum, send_n, recv_n, bits, me)]
        other = bits[:1] + bits[2:] + bits[1:2]
        streams.append(Stream(far, far_slots, far_sum, send_f, recv_f, other, me))
        streams[0].start(0)
        arrived_b[me] = source_b[me]
        exchange_wait(count, me, source_b, arrived_b, send_c, recv_c)
        mixed, flats = far_levels(count, depth, arrived_b, far_scratch, weight_ref, True)
        far_back(count, mixed, leaving_b, cols)
        part = jnp.sum(jnp.sum(arrived_b[...], axis=0), axis=0, keepdims=True)
        leaving_b[:, cols:] = jnp.broadcast_to(part[None], (count, leaving_b.shape[1] - cols, chans))
        exchange_start(count, me, leaving_b, landed_b, send_d, recv_d)
        for level, flat in enumerate(flats):
            first = offset(count, level)
            total = max(count >> (level + 1), 1)
            prior = far_coeff[first : first + total].astype(F32).reshape(total * cols, chans)
            far[level * tiles : (level + 1) * tiles] = outer(prior.astype(BF16), flat).reshape(
                tiles, 8, chans
            )
        streams[1].start(0)
        for index in range(max(len(stream.stages) for stream in streams)):
            for stream in streams:
                if index < len(stream.stages):
                    stream.finish(index)
                    stream.start(index + 1)
        exchange_wait(count, me, leaving_b, landed_b, send_d, recv_d)
        out_ref[...] = landed_b[:, 0:cols]
        gbias_ref[...] = jnp.sum(landed_b[:, cols : cols + 8], axis=0) * scale_all
        point = jnp.zeros((chans, chans), F32)
        for level in range(len(scales)):
            source, base = (near_sum, level) if level < depth else (far_sum, level - depth)
            raw = source[base * tiles : (base + 1) * tiles].reshape(chans, chans) * scales[level]
            mix_ref[level] = (raw * factors[level]).astype(BF16)
            point = point + raw
        point_ref[...] = (point * scale_all).astype(BF16)


def main_call(fields, cotangent, weights, bias, step, count, factors, scales, scale_all):
    rows, width, chans = fields.shape
    depth = rows.bit_length() - 1
    levels = weights.shape[0]
    blocks, cols = width // step, width // count
    tiles = chans // 8
    near, far = depth * tiles, (levels - depth) * tiles
    turns = count.bit_length() - 1
    row_shape, padded = (count, cols, chans), (count, cols + 8, chans)
    whole = lambda shape: pl.BlockSpec(shape, lambda i: (0,) * len(shape))
    rows_f32 = pltpu.VMEM(row_shape, F32)
    return pl.pallas_call(
        functools.partial(main_kernel, count, depth, factors, scales, scale_all),
        grid=(2 * blocks,),
        in_specs=[
            pl.BlockSpec((rows, step, chans), lambda i: (0, jnp.minimum(i, blocks - 1), 0)),
            pl.BlockSpec((rows, step, chans), lambda i: (0, jnp.maximum(i - blocks, 0), 0)),
            whole(weights.shape),
            whole(bias.shape),
        ],
        out_specs=(
            pl.BlockSpec((1, rows, step, chans), lambda i: (jnp.maximum(i - blocks, 0), 0, 0, 0)),
            whole(row_shape),
            whole(weights.shape),
            whole((chans, chans)),
            whole((8, chans)),
        ),
        out_shape=(
            jax.ShapeDtypeStruct((blocks, rows, step, chans), BF16),
            jax.ShapeDtypeStruct(row_shape, F32),
            jax.ShapeDtypeStruct(weights.shape, BF16),
            jax.ShapeDtypeStruct((chans, chans), BF16),
            jax.ShapeDtypeStruct((8, chans), F32),
        ),
        scratch_shapes=[
            pltpu.VMEM((blocks, rows, step, chans), BF16),
            pltpu.VMEM((blocks, rows, step, chans), F32),
            pltpu.VMEM(row_shape, BF16),
            pltpu.VMEM(row_shape, BF16),
            rows_f32, rows_f32, rows_f32, rows_f32,
            rows_f32, rows_f32, pltpu.VMEM(padded, F32), pltpu.VMEM(padded, F32),
            pltpu.VMEM((near, 8, chans), F32),
            pltpu.VMEM((slot_tiles(near, count), 8, chans), F32),
            pltpu.VMEM((near, 8, chans), F32),
            pltpu.VMEM((far, 8, chans), F32),
            pltpu.VMEM((slot_tiles(far, count), 8, chans), F32),
            pltpu.VMEM((far, 8, chans), F32),
        ]
        + [pltpu.SemaphoreType.DMA((count,))] * 8
        + [pltpu.SemaphoreType.DMA((2 * turns,))] * 4,
        compiler_params=pltpu.CompilerParams(
            dimension_semantics=("arbitrary",), collective_id=0, has_side_effects=True,
            vmem_limit_bytes=56 << 20,
        ),
    )(fields, cotangent, weights, bias)


def shards(fields, cotangent, point_weight, mix_weight, bias_vec):
    rows, width, chans = fields.shape
    depth = rows.bit_length() - 1
    count = lax.axis_size("gx")
    levels = mix_weight.shape[0]
    step = 32
    blocks = width // step
    scales = [2.0 ** -(level + 1) for level in range(levels - 1)] + [2.0 ** -(levels - 1)]
    scales = np.array(scales, np.float32)
    joined = mix_weight.astype(F32) + point_weight.astype(F32)[None]
    weights = (joined * scales[:, None, None]).astype(BF16)
    bias = jnp.broadcast_to(bias_vec.astype(F32)[None], (8, chans))

    field_spec = pl.BlockSpec((rows, step, chans), lambda i: (0, i, 0))
    coeff_spec = pl.BlockSpec((1, rows, step, chans), lambda i: (i, 0, 0, 0))
    row_spec = pl.BlockSpec((step, chans), lambda i: (i, 0))
    weight_spec = pl.BlockSpec((levels, chans, chans), lambda i: (0, 0, 0))
    params = pltpu.CompilerParams(
        dimension_semantics=("arbitrary",), vmem_limit_bytes=48 << 20
    )
    mixed_type = pltpu.VMEM((rows, step, chans), F32)

    total_rows = rows * count
    members = [width * total_rows / 2 ** (level + 1) for level in range(levels - 1)] + [width]
    factors = [1.0 / math.sqrt(value) for value in members]
    scale_all = 1.0 / math.sqrt(total_rows * width)
    backs, spectral_back, grad_mix, grad_point, grad_bias = main_call(
        fields, cotangent, weights, bias, step, count,
        factors, [float(value) for value in scales], scale_all,
    )

    (grad_input,) = pl.pallas_call(
        functools.partial(synth_kernel, depth),
        grid=(blocks,),
        in_specs=[coeff_spec, row_spec, weight_spec],
        out_specs=(field_spec,),
        out_shape=(jax.ShapeDtypeStruct(fields.shape, BF16),),
        scratch_shapes=[mixed_type],
        compiler_params=params,
        cost_estimate=pl.CostEstimate(
            flops=2 * rows * width * chans * chans, bytes_accessed=4 * rows * width * chans,
            transcendentals=0,
        ),
    )(backs, spectral_back.reshape(width, chans), weights)

    grad_bias = grad_bias[0].astype(BF16)
    return (grad_input, grad_mix, grad_point, grad_bias)


def solution(mesh):
    in_specs = (P("gx", "ga", None), P("gx", "ga", None), P(), P(), P())
    out_specs = (P("gx", "ga", None), P("ga", None, None), P("ga", None), P("ga"))
    return jax.shard_map(shards, mesh=mesh, in_specs=in_specs, out_specs=out_specs, check_vma=False)
```

```python
import functools
import math

import jax
import jax.numpy as jnp
from jax import lax
from jax.experimental import pallas as pl
from jax.experimental.pallas import tpu as pltpu
from jax.sharding import PartitionSpec as P

F32 = jnp.float32
BF16 = jnp.bfloat16
LANES = 16
GELU_K = math.sqrt(2.0 / math.pi)
GELU_C = 0.044715


def offset(rows, level):
    return rows - (rows >> level)


def outer(left, right):
    return lax.dot_general(left, right, (((0,), (0,)), ((), ())), preferred_element_type=F32)


def apply_weight(rows, weight, turned):
    sides = (((1,), (1 if turned else 0,)), ((), ()))
    return lax.dot_general(rows, weight, sides, preferred_element_type=F32)


def slope_of(value, cot):
    square = value * value
    inner = value * (GELU_K + (GELU_K * GELU_C) * square)
    half = 0.5 + 0.5 * jnp.tanh(inner)
    ramp = value * (2.0 * GELU_K + (6.0 * GELU_K * GELU_C) * square)
    return cot * (half * (1.0 + (1.0 - half) * ramp))


def join_weights(mix_ref, point_ref, scales, joined):
    point = point_ref[...].astype(F32)
    for level, scale in enumerate(scales):
        joined[level] = ((mix_ref[level].astype(F32) + point) * scale).astype(BF16)


def mix_block(depth, coeff_ref, weight_ref, mixed_ref, turned):
    rows = 1 << depth
    wide = coeff_ref.shape[1]
    for level in range(depth):
        first, count = offset(rows, level), rows >> (level + 1)
        flat = coeff_ref[first : first + count].reshape(count * wide, coeff_ref.shape[2])
        mixed_ref[first : first + count] = apply_weight(flat, weight_ref[level], turned).reshape(
            count, wide, weight_ref.shape[2]
        )


def synth_kernel(
    depth, scales, back_ref, coarse_ref, raw_mix_ref, raw_point_ref, out_ref, mixed_ref, weight_ref
):
    rows = 1 << depth

    @pl.when(pl.program_id(0) == 0)
    def _():
        join_weights(raw_mix_ref, raw_point_ref, scales, weight_ref)

    mix_block(depth, back_ref.at[0], weight_ref, mixed_ref, True)

    @pl.loop(0, back_ref.shape[2] // LANES)
    def _(sub):
        cols = pl.ds(pl.multiple_of(sub * LANES, LANES), LANES)

        def tree(level, index, value):
            if level == 0:
                out_ref[index, cols, :] = value.astype(BF16)
                return
            detail = mixed_ref[offset(rows, level - 1) + index, cols, :]
            tree(level - 1, 2 * index, value - detail)
            tree(level - 1, 2 * index + 1, value + detail)

        tree(depth, 0, coarse_ref[cols, :])


class Stream:
    def __init__(self, total, slots, result, send, recv, bits, me):
        self.total, self.slots, self.result = total, slots, result
        self.send, self.recv = send, recv
        start, length, place = 0, total.shape[0], 0
        self.plan = []
        for turn, bit in enumerate(bits):
            upper = lax.rem(me // (1 << bit), 2)
            partner = me + (1 - 2 * upper) * (1 << bit)
            halved = length % 2 == 0
            size = length // 2 if halved else length
            keep = start + upper * size if halved else start
            give = start + (1 - upper) * size if halved else start
            self.plan.append((turn, partner, halved, size, keep, give, place))
            start, length, place = keep, size, place + size
        self.stages = [("sum",) + item for item in self.plan]
        self.stages += [("spread",) + item for item in self.plan[::-1] if item[2]]

    def copy(self, index):
        kind, turn, partner, halved, size, keep, give, place = self.stages[index]
        if kind == "sum":
            source = self.total.at[pl.ds(give, size)]
            target = self.slots.at[pl.ds(place, size)]
        else:
            source = self.result.at[pl.ds(keep, size)]
            target = self.result.at[pl.ds(keep, size)]
        return pltpu.make_async_remote_copy(
            src_ref=source,
            dst_ref=target,
            send_sem=self.send.at[index],
            recv_sem=self.recv.at[index],
            device_id={"gx": partner},
            device_id_type=pl.DeviceIdType.MESH,
        )

    def start(self, index):
        if index < len(self.stages):
            self.copy(index).start()

    def finish(self, index):
        self.copy(index).wait()
        kind, turn, partner, halved, size, keep, give, place = self.stages[index]
        if kind == "sum":
            here = pl.ds(keep, size)
            into = self.result if turn == len(self.plan) - 1 else self.total
            into[here] = self.total[here] + self.slots[pl.ds(place, size)]


def slot_tiles(tiles, count):
    used = 0
    for _ in range(count.bit_length() - 1):
        tiles = tiles // 2 if tiles % 2 == 0 else tiles
        used += tiles
    return used


def far_levels(count, first_level, arrived, coeff_ref, weight_ref, turned):
    depth = count.bit_length() - 1
    cols, chans = arrived.shape[1], arrived.shape[2]

    def down(level, index):
        if level == 0:
            return arrived[index]
        even = down(level - 1, 2 * index)
        odd = down(level - 1, 2 * index + 1)
        coeff_ref[offset(count, level - 1) + index] = (odd - even).astype(BF16)
        return even + odd

    coeff_ref[count - 1] = down(depth, 0).astype(BF16)
    mixed, flats = [], []
    for level in range(depth + 1):
        first = offset(count, level)
        total = max(count >> (level + 1), 1)
        flat = coeff_ref[first : first + total].astype(F32).reshape(total * cols, chans).astype(BF16)
        flats.append(flat)
        mixed.append(
            apply_weight(flat, weight_ref[first_level + level], turned).reshape(total, cols, chans)
        )
    return mixed, flats


def far_back(count, mixed, leaving, cols):
    depth = count.bit_length() - 1

    def up(level, index, value):
        if level == 0:
            leaving[index, 0:cols] = value
            return
        detail = mixed[level - 1][index]
        up(level - 1, 2 * index, value - detail)
        up(level - 1, 2 * index + 1, value + detail)

    up(depth, 0, mixed[depth][0])


def swap(count, me, source, target, send, recv, step):
    peer = lax.rem(me + step, count)
    return pltpu.make_async_remote_copy(
        src_ref=source.at[peer],
        dst_ref=target.at[me],
        send_sem=send.at[step],
        recv_sem=recv.at[step],
        device_id={"gx": peer},
        device_id_type=pl.DeviceIdType.MESH,
    )


def exchange_start(count, me, source, target, send, recv):
    @pl.loop(1, count)
    def _(step):
        swap(count, me, source, target, send, recv, step).start()

    target[me] = source[me]


def exchange_wait(count, me, source, target, send, recv):
    @pl.loop(1, count)
    def _(step):
        swap(count, me, source, target, send, recv, step).wait()


def send_block(count, me, block, share, source, target, send, recv):
    @pl.loop(0, share)
    def _(turn):
        step = lax.rem(block * share + turn - me + count, count)

        @pl.when(step > 0)
        def _():
            swap(count, me, source, target, send, recv, step).start()


def main_kernel(
    count, depth, factors, scales, scale_all,
    fields_ref, cot_ref, raw_mix_ref, raw_point_ref, bias_ref,
    back_ref, out_ref, mix_ref, point_ref, gbias_ref,
    weight_ref, coeff, mixed_all, far_coeff, far_scratch,
    source_a, arrived_a, leaving_a, landed_a,
    source_b, arrived_b, leaving_b, landed_b,
    near, near_slots, near_sum, far, far_slots, far_sum,
    send_a, recv_a, send_b, recv_b, send_c, recv_c, send_d, recv_d,
    send_n, recv_n, send_f, recv_f,
):
    me = lax.axis_index("gx")
    turn = pl.program_id(0)
    blocks, rows, wide, chans = coeff.shape
    cols = source_a.shape[1]
    tiles = chans // 8
    share, piece = wide // cols, LANES // cols
    bits = list(range(count.bit_length() - 1))
    barrier = pltpu.get_barrier_semaphore()

    @pl.when(turn == 0)
    def _():
        @pl.loop(1, count)
        def _(step):
            pl.semaphore_signal(
                barrier,
                inc=1,
                device_id={"gx": lax.rem(me + step, count)},
                device_id_type=pl.DeviceIdType.MESH,
            )

        near[...] = jnp.zeros_like(near)
        join_weights(raw_mix_ref, raw_point_ref, scales, weight_ref)

    @pl.when(turn < blocks)
    def _():
        @pl.loop(0, wide // LANES)
        def _(sub):
            here = pl.ds(pl.multiple_of(sub * LANES, LANES), LANES)

            def tree(level, index):
                if level == 0:
                    return fields_ref[index, here, :].astype(F32)
                even = tree(level - 1, 2 * index)
                odd = tree(level - 1, 2 * index + 1)
                coeff[turn, offset(rows, level - 1) + index, here, :] = (odd - even).astype(BF16)
                return even + odd

            source_a[pl.ds(turn * share + sub * piece, piece)] = tree(depth, 0).reshape(
                piece, cols, chans
            )

        @pl.when(turn == 0)
        def _():
            pl.semaphore_wait(barrier, count - 1)

        send_block(count, me, turn, share, source_a, arrived_a, send_a, recv_a)

    @pl.when(turn == blocks)
    def _():
        @pl.loop(0, blocks // 2)
        def _(block):
            mix_block(depth, coeff.at[block], weight_ref, mixed_all.at[block], False)

        arrived_a[me] = source_a[me]
        exchange_wait(count, me, source_a, arrived_a, send_a, recv_a)
        mixed, _ = far_levels(count, depth, arrived_a, far_coeff, weight_ref, False)
        far_back(count, mixed, leaving_a, cols)
        exchange_start(count, me, leaving_a, landed_a, send_b, recv_b)

        @pl.loop(blocks // 2, blocks)
        def _(block):
            mix_block(depth, coeff.at[block], weight_ref, mixed_all.at[block], False)

        exchange_wait(count, me, leaving_a, landed_a, send_b, recv_b)

    @pl.when(turn >= blocks)
    def _():
        block = turn - blocks

        @pl.loop(0, wide // LANES)
        def _(sub):
            here = pl.ds(pl.multiple_of(sub * LANES, LANES), LANES)

            def tree(level, index, value):
                if level == 0:
                    cot = cot_ref[index, here, :].astype(F32)
                    return slope_of(value, cot).astype(BF16).astype(F32)
                place = offset(rows, level - 1) + index
                detail = mixed_all[block, place, here, :]
                even = tree(level - 1, 2 * index, value - detail)
                odd = tree(level - 1, 2 * index + 1, value + detail)
                back_ref[0, place, here, :] = (odd - even).astype(BF16)
                return even + odd

            pieces = pl.ds(block * share + sub * piece, piece)
            start = landed_a[pieces].reshape(LANES, chans) + bias_ref[...].astype(F32)
            source_b[pieces] = tree(depth, 0, start).reshape(piece, cols, chans)

        send_block(count, me, block, share, source_b, arrived_b, send_c, recv_c)
        for level in range(depth):
            first, number = offset(rows, level), rows >> (level + 1)
            left = coeff[block, first : first + number].reshape(number * wide, chans)
            right = back_ref[0, first : first + number].reshape(number * wide, chans)
            near[level * tiles : (level + 1) * tiles] += outer(left, right).reshape(tiles, 8, chans)

    @pl.when(turn == 2 * blocks - 1)
    def _():
        streams = [Stream(near, near_slots, near_sum, send_n, recv_n, bits, me)]
        other = bits[:1] + bits[2:] + bits[1:2]
        streams.append(Stream(far, far_slots, far_sum, send_f, recv_f, other, me))
        streams[0].start(0)
        arrived_b[me] = source_b[me]
        streams[0].finish(0)
        streams[0].start(1)
        exchange_wait(count, me, source_b, arrived_b, send_c, recv_c)
        mixed, flats = far_levels(count, depth, arrived_b, far_scratch, weight_ref, True)
        far_back(count, mixed, leaving_b, cols)
        part = jnp.sum(jnp.sum(arrived_b[...], axis=0), axis=0, keepdims=True)
        leaving_b[:, cols:] = jnp.broadcast_to(part[None], (count, leaving_b.shape[1] - cols, chans))
        exchange_start(count, me, leaving_b, landed_b, send_d, recv_d)
        for level, flat in enumerate(flats):
            first = offset(count, level)
            total = max(count >> (level + 1), 1)
            prior = far_coeff[first : first + total].astype(F32).reshape(total * cols, chans)
            far[level * tiles : (level + 1) * tiles] = outer(prior.astype(BF16), flat).reshape(
                tiles, 8, chans
            )
        streams[1].start(0)
        for index in range(max(len(stream.stages) for stream in streams)):
            for stream, stage in ((streams[1], index), (streams[0], index + 1)):
                if stage < len(stream.stages):
                    stream.finish(stage)
                    stream.start(stage + 1)
        exchange_wait(count, me, leaving_b, landed_b, send_d, recv_d)
        out_ref[...] = landed_b[:, 0:cols]
        gbias_ref[...] = jnp.sum(landed_b[:, cols : cols + 8], axis=0) * scale_all
        point = jnp.zeros((chans, chans), F32)
        for level in range(len(scales)):
            source, base = (near_sum, level) if level < depth else (far_sum, level - depth)
            raw = source[base * tiles : (base + 1) * tiles].reshape(chans, chans) * scales[level]
            mix_ref[level] = (raw * factors[level]).astype(BF16)
            point = point + raw
        point_ref[...] = (point * scale_all).astype(BF16)


def main_call(fields, cotangent, weights, point_weight, bias, step, count, factors, scales, scale_all):
    rows, width, chans = fields.shape
    depth = rows.bit_length() - 1
    levels = weights.shape[0]
    blocks, cols = width // step, width // count
    tiles = chans // 8
    near, far = depth * tiles, (levels - depth) * tiles
    turns = count.bit_length() - 1
    row_shape, padded = (count, cols, chans), (count, cols + 8, chans)
    whole = lambda shape: pl.BlockSpec(shape, lambda i: (0,) * len(shape))
    rows_f32 = pltpu.VMEM(row_shape, F32)
    return pl.pallas_call(
        functools.partial(main_kernel, count, depth, factors, scales, scale_all),
        grid=(2 * blocks,),
        in_specs=[
            pl.BlockSpec((rows, step, chans), lambda i: (0, jnp.minimum(i, blocks - 1), 0)),
            pl.BlockSpec((rows, step, chans), lambda i: (0, jnp.maximum(i - blocks, 0), 0)),
            whole(weights.shape),
            whole(point_weight.shape),
            whole(bias.shape),
        ],
        out_specs=(
            pl.BlockSpec((1, rows, step, chans), lambda i: (jnp.maximum(i - blocks, 0), 0, 0, 0)),
            whole(row_shape),
            whole(weights.shape),
            whole((chans, chans)),
            whole((8, chans)),
        ),
        out_shape=(
            jax.ShapeDtypeStruct((blocks, rows, step, chans), BF16),
            jax.ShapeDtypeStruct(row_shape, F32),
            jax.ShapeDtypeStruct(weights.shape, BF16),
            jax.ShapeDtypeStruct((chans, chans), BF16),
            jax.ShapeDtypeStruct((8, chans), F32),
        ),
        scratch_shapes=[
            pltpu.VMEM(weights.shape, BF16),
            pltpu.VMEM((blocks, rows, step, chans), BF16),
            pltpu.VMEM((blocks, rows, step, chans), F32),
            pltpu.VMEM(row_shape, BF16),
            pltpu.VMEM(row_shape, BF16),
            rows_f32, rows_f32, rows_f32, rows_f32,
            rows_f32, rows_f32, pltpu.VMEM(padded, F32), pltpu.VMEM(padded, F32),
            pltpu.VMEM((near, 8, chans), F32),
            pltpu.VMEM((slot_tiles(near, count), 8, chans), F32),
            pltpu.VMEM((near, 8, chans), F32),
            pltpu.VMEM((far, 8, chans), F32),
            pltpu.VMEM((slot_tiles(far, count), 8, chans), F32),
            pltpu.VMEM((far, 8, chans), F32),
        ]
        + [pltpu.SemaphoreType.DMA((count,))] * 8
        + [pltpu.SemaphoreType.DMA((2 * turns,))] * 4,
        compiler_params=pltpu.CompilerParams(
            dimension_semantics=("arbitrary",), collective_id=0, has_side_effects=True,
            vmem_limit_bytes=56 << 20,
        ),
    )(fields, cotangent, weights, point_weight, bias)


def shards(fields, cotangent, point_weight, mix_weight, bias_vec):
    rows, width, chans = fields.shape
    depth = rows.bit_length() - 1
    count = lax.axis_size("gx")
    levels = mix_weight.shape[0]
    step = 32
    blocks = width // step
    scales = [2.0 ** -(level + 1) for level in range(levels - 1)] + [2.0 ** -(levels - 1)]
    bias = bias_vec.reshape(1, chans)

    field_spec = pl.BlockSpec((rows, step, chans), lambda i: (0, i, 0))
    coeff_spec = pl.BlockSpec((1, rows, step, chans), lambda i: (i, 0, 0, 0))
    row_spec = pl.BlockSpec((step, chans), lambda i: (i, 0))
    weight_spec = pl.BlockSpec((levels, chans, chans), lambda i: (0, 0, 0))
    params = pltpu.CompilerParams(
        dimension_semantics=("arbitrary",), vmem_limit_bytes=48 << 20
    )
    mixed_type = pltpu.VMEM((rows, step, chans), F32)

    total_rows = rows * count
    members = [width * total_rows / 2 ** (level + 1) for level in range(levels - 1)] + [width]
    factors = [1.0 / math.sqrt(value) for value in members]
    scale_all = 1.0 / math.sqrt(total_rows * width)
    backs, spectral_back, grad_mix, grad_point, grad_bias = main_call(
        fields, cotangent, mix_weight, point_weight, bias, step, count, factors, scales, scale_all,
    )

    (grad_input,) = pl.pallas_call(
        functools.partial(synth_kernel, depth, scales),
        grid=(blocks,),
        in_specs=[
            coeff_spec, row_spec, weight_spec,
            pl.BlockSpec(point_weight.shape, lambda i: (0, 0)),
        ],
        out_specs=(field_spec,),
        out_shape=(jax.ShapeDtypeStruct(fields.shape, BF16),),
        scratch_shapes=[mixed_type, pltpu.VMEM(mix_weight.shape, BF16)],
        compiler_params=params,
        cost_estimate=pl.CostEstimate(
            flops=2 * rows * width * chans * chans, bytes_accessed=4 * rows * width * chans,
            transcendentals=0,
        ),
    )(backs, spectral_back.reshape(width, chans), mix_weight, point_weight)

    grad_bias = grad_bias[0].astype(BF16)
    return (grad_input, grad_mix, grad_point, grad_bias)


def solution(mesh):
    in_specs = (P("gx", "ga", None), P("gx", "ga", None), P(), P(), P())
    out_specs = (P("gx", "ga", None), P("ga", None, None), P("ga", None), P("ga"))
    return jax.shard_map(shards, mesh=mesh, in_specs=in_specs, out_specs=out_specs, check_vma=False)
```

```python
import functools
import math

import jax
import jax.numpy as jnp
from jax import lax
from jax.experimental import pallas as pl
from jax.experimental.pallas import tpu as pltpu
from jax.sharding import PartitionSpec as P

F32 = jnp.float32
BF16 = jnp.bfloat16
LANES = 16
GELU_K = math.sqrt(2.0 / math.pi)
GELU_C = 0.044715


def offset(rows, level):
    return rows - (rows >> level)


def outer(left, right):
    return lax.dot_general(left, right, (((0,), (0,)), ((), ())), preferred_element_type=F32)


def apply_weight(rows, weight, turned):
    sides = (((1,), (1 if turned else 0,)), ((), ()))
    return lax.dot_general(rows, weight, sides, preferred_element_type=F32)


def slope_of(value, cot):
    square = value * value
    inner = value * (GELU_K + (GELU_K * GELU_C) * square)
    half = 0.5 + 0.5 * jnp.tanh(inner)
    ramp = value * (2.0 * GELU_K + (6.0 * GELU_K * GELU_C) * square)
    return cot * (half * (1.0 + (1.0 - half) * ramp))


def join_weights(mix_ref, point_ref, scales, joined):
    point = point_ref[...].astype(F32)
    for level, scale in enumerate(scales):
        joined[level] = ((mix_ref[level].astype(F32) + point) * scale).astype(BF16)


def mix_block(depth, coeff_ref, weight_ref, mixed_ref, turned):
    rows = 1 << depth
    wide = coeff_ref.shape[1]
    for level in range(depth):
        first, count = offset(rows, level), rows >> (level + 1)
        flat = coeff_ref[first : first + count].reshape(count * wide, coeff_ref.shape[2])
        mixed_ref[first : first + count] = apply_weight(flat, weight_ref[level], turned).reshape(
            count, wide, weight_ref.shape[2]
        )


def synth_kernel(
    depth, scales, back_ref, coarse_ref, raw_mix_ref, raw_point_ref, out_ref, mixed_ref, weight_ref
):
    rows = 1 << depth

    @pl.when(pl.program_id(0) == 0)
    def _():
        join_weights(raw_mix_ref, raw_point_ref, scales, weight_ref)

    mix_block(depth, back_ref.at[0], weight_ref, mixed_ref, True)

    @pl.loop(0, back_ref.shape[2] // LANES)
    def _(sub):
        cols = pl.ds(pl.multiple_of(sub * LANES, LANES), LANES)

        def tree(level, index, value):
            if level == 0:
                out_ref[index, cols, :] = value.astype(BF16)
                return
            detail = mixed_ref[offset(rows, level - 1) + index, cols, :]
            tree(level - 1, 2 * index, value - detail)
            tree(level - 1, 2 * index + 1, value + detail)

        tree(depth, 0, coarse_ref[cols, :])


class Stream:
    def __init__(self, total, slots, result, send, recv, bits, me):
        self.total, self.slots, self.result = total, slots, result
        self.send, self.recv = send, recv
        start, length, place = 0, total.shape[0], 0
        self.plan = []
        for turn, bit in enumerate(bits):
            upper = lax.rem(me // (1 << bit), 2)
            partner = me + (1 - 2 * upper) * (1 << bit)
            halved = length % 2 == 0
            size = length // 2 if halved else length
            keep = start + upper * size if halved else start
            give = start + (1 - upper) * size if halved else start
            self.plan.append((turn, partner, halved, size, keep, give, place))
            start, length, place = keep, size, place + size
        self.stages = [("sum",) + item for item in self.plan]
        self.stages += [("spread",) + item for item in self.plan[::-1] if item[2]]

    def copy(self, index):
        kind, turn, partner, halved, size, keep, give, place = self.stages[index]
        if kind == "sum":
            source = self.total.at[pl.ds(give, size)]
            target = self.slots.at[pl.ds(place, size)]
        else:
            source = self.result.at[pl.ds(keep, size)]
            target = self.result.at[pl.ds(keep, size)]
        return pltpu.make_async_remote_copy(
            src_ref=source,
            dst_ref=target,
            send_sem=self.send.at[index],
            recv_sem=self.recv.at[index],
            device_id={"gx": partner},
            device_id_type=pl.DeviceIdType.MESH,
        )

    def start(self, index):
        if index < len(self.stages):
            self.copy(index).start()

    def finish(self, index):
        self.copy(index).wait()
        kind, turn, partner, halved, size, keep, give, place = self.stages[index]
        if kind == "sum":
            here = pl.ds(keep, size)
            into = self.result if turn == len(self.plan) - 1 else self.total
            into[here] = self.total[here] + self.slots[pl.ds(place, size)]


def slot_tiles(tiles, count):
    used = 0
    for _ in range(count.bit_length() - 1):
        tiles = tiles // 2 if tiles % 2 == 0 else tiles
        used += tiles
    return used


def far_levels(count, first_level, arrived, coeff_ref, weight_ref, turned):
    depth = count.bit_length() - 1
    cols, chans = arrived.shape[1], arrived.shape[2]

    def down(level, index):
        if level == 0:
            return arrived[index]
        even = down(level - 1, 2 * index)
        odd = down(level - 1, 2 * index + 1)
        coeff_ref[offset(count, level - 1) + index] = (odd - even).astype(BF16)
        return even + odd

    coeff_ref[count - 1] = down(depth, 0).astype(BF16)
    mixed, flats = [], []
    for level in range(depth + 1):
        first = offset(count, level)
        total = max(count >> (level + 1), 1)
        flat = coeff_ref[first : first + total].astype(F32).reshape(total * cols, chans).astype(BF16)
        flats.append(flat)
        mixed.append(
            apply_weight(flat, weight_ref[first_level + level], turned).reshape(total, cols, chans)
        )
    return mixed, flats


def far_back(count, mixed, leaving, cols):
    depth = count.bit_length() - 1

    def up(level, index, value):
        if level == 0:
            leaving[index, 0:cols] = value
            return
        detail = mixed[level - 1][index]
        up(level - 1, 2 * index, value - detail)
        up(level - 1, 2 * index + 1, value + detail)

    up(depth, 0, mixed[depth][0])


def swap(count, me, source, target, send, recv, step):
    peer = lax.rem(me + step, count)
    return pltpu.make_async_remote_copy(
        src_ref=source.at[peer],
        dst_ref=target.at[me],
        send_sem=send.at[step],
        recv_sem=recv.at[step],
        device_id={"gx": peer},
        device_id_type=pl.DeviceIdType.MESH,
    )


def exchange_start(count, me, source, target, send, recv):
    @pl.loop(1, count)
    def _(step):
        swap(count, me, source, target, send, recv, step).start()

    target[me] = source[me]


def exchange_wait(count, me, source, target, send, recv):
    @pl.loop(1, count)
    def _(step):
        swap(count, me, source, target, send, recv, step).wait()


def send_block(count, me, block, share, source, target, send, recv):
    @pl.loop(0, share)
    def _(turn):
        step = lax.rem(block * share + turn - me + count, count)

        @pl.when(step > 0)
        def _():
            swap(count, me, source, target, send, recv, step).start()


def main_kernel(
    count, depth, factors, scales, scale_all,
    fields_ref, cot_ref, raw_mix_ref, raw_point_ref, bias_ref,
    back_ref, out_ref, mix_ref, point_ref, gbias_ref,
    weight_ref, coeff, mixed_all, far_coeff, far_scratch,
    source_a, arrived_a, leaving_a, landed_a,
    source_b, arrived_b, leaving_b, landed_b,
    near, near_slots, near_sum, far, far_slots, far_sum,
    send_a, recv_a, send_b, recv_b, send_c, recv_c, send_d, recv_d,
    send_n, recv_n, send_f, recv_f,
):
    me = lax.axis_index("gx")
    turn = pl.program_id(0)
    blocks, rows, wide, chans = coeff.shape
    cols = source_a.shape[1]
    tiles = chans // 8
    share, piece = wide // cols, LANES // cols
    bits = list(range(count.bit_length() - 1))
    barrier = pltpu.get_barrier_semaphore()

    @pl.when(turn == 0)
    def _():
        @pl.loop(1, count)
        def _(step):
            pl.semaphore_signal(
                barrier,
                inc=1,
                device_id={"gx": lax.rem(me + step, count)},
                device_id_type=pl.DeviceIdType.MESH,
            )

        near[...] = jnp.zeros_like(near)
        join_weights(raw_mix_ref, raw_point_ref, scales, weight_ref)

    @pl.when(turn < blocks)
    def _():
        @pl.loop(0, wide // LANES)
        def _(sub):
            here = pl.ds(pl.multiple_of(sub * LANES, LANES), LANES)

            def tree(level, index):
                if level == 0:
                    return fields_ref[index, here, :].astype(F32)
                even = tree(level - 1, 2 * index)
                odd = tree(level - 1, 2 * index + 1)
                coeff[turn, offset(rows, level - 1) + index, here, :] = (odd - even).astype(BF16)
                return even + odd

            source_a[pl.ds(turn * share + sub * piece, piece)] = tree(depth, 0).reshape(
                piece, cols, chans
            )

        @pl.when(turn == 0)
        def _():
            pl.semaphore_wait(barrier, count - 1)

        send_block(count, me, turn, share, source_a, arrived_a, send_a, recv_a)

    @pl.when(turn == blocks)
    def _():
        @pl.loop(0, blocks // 2)
        def _(block):
            mix_block(depth, coeff.at[block], weight_ref, mixed_all.at[block], False)

        arrived_a[me] = source_a[me]
        exchange_wait(count, me, source_a, arrived_a, send_a, recv_a)
        mixed, _ = far_levels(count, depth, arrived_a, far_coeff, weight_ref, False)
        far_back(count, mixed, leaving_a, cols)
        exchange_start(count, me, leaving_a, landed_a, send_b, recv_b)

        @pl.loop(blocks // 2, blocks)
        def _(block):
            mix_block(depth, coeff.at[block], weight_ref, mixed_all.at[block], False)

        exchange_wait(count, me, leaving_a, landed_a, send_b, recv_b)

    @pl.when(turn >= blocks)
    def _():
        block = turn - blocks

        @pl.loop(0, wide // LANES)
        def _(sub):
            here = pl.ds(pl.multiple_of(sub * LANES, LANES), LANES)

            def tree(level, index, value):
                if level == 0:
                    cot = cot_ref[index, here, :].astype(F32)
                    return slope_of(value, cot).astype(BF16).astype(F32)
                place = offset(rows, level - 1) + index
                detail = mixed_all[block, place, here, :]
                even = tree(level - 1, 2 * index, value - detail)
                odd = tree(level - 1, 2 * index + 1, value + detail)
                back_ref[0, place, here, :] = (odd - even).astype(BF16)
                return even + odd

            pieces = pl.ds(block * share + sub * piece, piece)
            start = landed_a[pieces].reshape(LANES, chans) + bias_ref[...].astype(F32)
            source_b[pieces] = tree(depth, 0, start).reshape(piece, cols, chans)

        send_block(count, me, block, share, source_b, arrived_b, send_c, recv_c)
        for level in range(depth):
            first, number = offset(rows, level), rows >> (level + 1)
            left = coeff[block, first : first + number].reshape(number * wide, chans)
            right = back_ref[0, first : first + number].reshape(number * wide, chans)
            near[level * tiles : (level + 1) * tiles] += outer(left, right).reshape(tiles, 8, chans)

    @pl.when(turn == 2 * blocks - 1)
    def _():
        streams = [Stream(near, near_slots, near_sum, send_n, recv_n, bits, me)]
        other = bits[:1] + bits[2:] + bits[1:2]
        streams.append(Stream(far, far_slots, far_sum, send_f, recv_f, other, me))
        streams[0].start(0)
        arrived_b[me] = source_b[me]
        streams[0].finish(0)
        streams[0].start(1)
        exchange_wait(count, me, source_b, arrived_b, send_c, recv_c)
        mixed, flats = far_levels(count, depth, arrived_b, far_scratch, weight_ref, True)
        far_back(count, mixed, leaving_b, cols)
        part = jnp.sum(jnp.sum(arrived_b[...], axis=0), axis=0, keepdims=True)
        leaving_b[:, cols:] = jnp.broadcast_to(part[None], (count, leaving_b.shape[1] - cols, chans))
        exchange_start(count, me, leaving_b, landed_b, send_d, recv_d)
        for level, flat in enumerate(flats):
            first = offset(count, level)
            total = max(count >> (level + 1), 1)
            prior = far_coeff[first : first + total].astype(F32).reshape(total * cols, chans)
            far[level * tiles : (level + 1) * tiles] = outer(prior.astype(BF16), flat).reshape(
                tiles, 8, chans
            )
        streams[1].start(0)
        for index in range(max(len(stream.stages) for stream in streams)):
            for stream, stage in ((streams[1], index), (streams[0], index + 1)):
                if stage < len(stream.stages):
                    stream.finish(stage)
                    stream.start(stage + 1)
        exchange_wait(count, me, leaving_b, landed_b, send_d, recv_d)
        out_ref[...] = landed_b[:, 0:cols]
        gbias_ref[...] = jnp.sum(landed_b[:, cols : cols + 8], axis=0) * scale_all
        point = jnp.zeros((chans, chans), F32)
        for level in range(len(scales)):
            source, base = (near_sum, level) if level < depth else (far_sum, level - depth)
            raw = source[base * tiles : (base + 1) * tiles].reshape(chans, chans) * scales[level]
            mix_ref[level] = (raw * factors[level]).astype(BF16)
            point = point + raw
        point_ref[...] = (point * scale_all).astype(BF16)


def main_call(fields, cotangent, weights, point_weight, bias, step, count, factors, scales, scale_all):
    rows, width, chans = fields.shape
    depth = rows.bit_length() - 1
    levels = weights.shape[0]
    blocks, cols = width // step, width // count
    tiles = chans // 8
    near, far = depth * tiles, (levels - depth) * tiles
    turns = count.bit_length() - 1
    row_shape, padded = (count, cols, chans), (count, cols + 8, chans)
    whole = lambda shape: pl.BlockSpec(shape, lambda i: (0,) * len(shape))
    rows_f32 = pltpu.VMEM(row_shape, F32)
    return pl.pallas_call(
        functools.partial(main_kernel, count, depth, factors, scales, scale_all),
        grid=(2 * blocks,),
        in_specs=[
            pl.BlockSpec((rows, step, chans), lambda i: (0, jnp.minimum(i, blocks - 1), 0)),
            pl.BlockSpec((rows, step, chans), lambda i: (0, jnp.maximum(i - blocks, 0), 0)),
            whole(weights.shape),
            whole(point_weight.shape),
            whole(bias.shape),
        ],
        out_specs=(
            pl.BlockSpec((1, rows, step, chans), lambda i: (jnp.maximum(i - blocks, 0), 0, 0, 0)),
            whole(row_shape),
            whole(weights.shape),
            whole((chans, chans)),
            whole((8, chans)),
        ),
        out_shape=(
            jax.ShapeDtypeStruct((blocks, rows, step, chans), BF16),
            jax.ShapeDtypeStruct(row_shape, F32),
            jax.ShapeDtypeStruct(weights.shape, BF16),
            jax.ShapeDtypeStruct((chans, chans), BF16),
            jax.ShapeDtypeStruct((8, chans), F32),
        ),
        scratch_shapes=[
            pltpu.VMEM(weights.shape, BF16),
            pltpu.VMEM((blocks, rows, step, chans), BF16),
            pltpu.VMEM((blocks, rows, step, chans), F32),
            pltpu.VMEM(row_shape, BF16),
            pltpu.VMEM(row_shape, BF16),
            rows_f32, rows_f32, rows_f32, rows_f32,
            rows_f32, rows_f32, pltpu.VMEM(padded, F32), pltpu.VMEM(padded, F32),
            pltpu.VMEM((near, 8, chans), F32),
            pltpu.VMEM((slot_tiles(near, count), 8, chans), F32),
            pltpu.VMEM((near, 8, chans), F32),
            pltpu.VMEM((far, 8, chans), F32),
            pltpu.VMEM((slot_tiles(far, count), 8, chans), F32),
            pltpu.VMEM((far, 8, chans), F32),
        ]
        + [pltpu.SemaphoreType.DMA((count,))] * 8
        + [pltpu.SemaphoreType.DMA((2 * turns,))] * 4,
        compiler_params=pltpu.CompilerParams(
            dimension_semantics=("arbitrary",), collective_id=0, has_side_effects=True,
            vmem_limit_bytes=56 << 20,
        ),
    )(fields, cotangent, weights, point_weight, bias)


def shards(fields, cotangent, point_weight, mix_weight, bias_vec):
    rows, width, chans = fields.shape
    depth = rows.bit_length() - 1
    count = lax.axis_size("gx")
    levels = mix_weight.shape[0]
    step = 64
    blocks = width // step
    scales = [2.0 ** -(level + 1) for level in range(levels - 1)] + [2.0 ** -(levels - 1)]
    bias = bias_vec.reshape(1, chans)

    field_spec = pl.BlockSpec((rows, step, chans), lambda i: (0, i, 0))
    coeff_spec = pl.BlockSpec((1, rows, step, chans), lambda i: (i, 0, 0, 0))
    row_spec = pl.BlockSpec((step, chans), lambda i: (i, 0))
    weight_spec = pl.BlockSpec((levels, chans, chans), lambda i: (0, 0, 0))
    params = pltpu.CompilerParams(
        dimension_semantics=("arbitrary",), vmem_limit_bytes=48 << 20
    )
    mixed_type = pltpu.VMEM((rows, step, chans), F32)

    total_rows = rows * count
    members = [width * total_rows / 2 ** (level + 1) for level in range(levels - 1)] + [width]
    factors = [1.0 / math.sqrt(value) for value in members]
    scale_all = 1.0 / math.sqrt(total_rows * width)
    backs, spectral_back, grad_mix, grad_point, grad_bias = main_call(
        fields, cotangent, mix_weight, point_weight, bias, step, count, factors, scales, scale_all,
    )

    (grad_input,) = pl.pallas_call(
        functools.partial(synth_kernel, depth, scales),
        grid=(blocks,),
        in_specs=[
            coeff_spec, row_spec, weight_spec,
            pl.BlockSpec(point_weight.shape, lambda i: (0, 0)),
        ],
        out_specs=(field_spec,),
        out_shape=(jax.ShapeDtypeStruct(fields.shape, BF16),),
        scratch_shapes=[mixed_type, pltpu.VMEM(mix_weight.shape, BF16)],
        compiler_params=params,
        cost_estimate=pl.CostEstimate(
            flops=2 * rows * width * chans * chans, bytes_accessed=4 * rows * width * chans,
            transcendentals=0,
        ),
    )(backs, spectral_back.reshape(width, chans), mix_weight, point_weight)

    grad_bias = grad_bias[0].astype(BF16)
    return (grad_input, grad_mix, grad_point, grad_bias)


def solution(mesh):
    in_specs = (P("gx", "ga", None), P("gx", "ga", None), P(), P(), P())
    out_specs = (P("gx", "ga", None), P("ga", None, None), P("ga", None), P("ga"))
    return jax.shard_map(shards, mesh=mesh, in_specs=in_specs, out_specs=out_specs, check_vma=False)
```
